256 devices in a mesh: ctx: 32 (over z_hi, x, core), exp: 8 (over z_lo, y).
Axes of the slice: x: 4, y: 4, z: 8 (z_hi: 4, z_lo: 2; z = z_hi * 2 + z_lo), core: 2. Of those that a mesh axis runs over, the one named last changes fastest.
Arguments:
- hidden_acts: bfloat16 [64, 32, 16, 2048], P('ctx', None, None, 'exp'), may hold values from -6 to 6
- down_weight: bfloat16 [64, 2048, 2880], P('ctx', 'exp'), may hold values from -0.125 to 0.125
- expert_ids: int32 [4096, 4], P('ctx'), may hold values from 0 to 63, all different within a row; in each aligned block of 128 rows (0 to 127, 128 to 255, ...) at most 16 rows name the same one
- route_logits: float32 [4096, 4], P('ctx'), may hold values from -4 to 4
- out_grad: bfloat16 [4096, 2880], P('ctx', 'exp'), may hold values from -6 to 6
Outputs:
- combined: bfloat16 [4096, 2880], P('ctx', 'exp')
- grad_logits: float32 [4096, 4], P('ctx')
- grad_hidden: bfloat16 [64, 32, 16, 2048], P('ctx', None, None, 'exp')
- grad_weight: bfloat16 [64, 2048, 2880], P('ctx', 'exp')
The draws below stay inside these ranges and needn't reach their ends.
Inputs may be any that keep to these rules, and one draw needn't show every extreme that they name: `expert_ids`: each token names 4 different experts; within each aligned block of 128 tokens no expert is named by more than 16 tokens, a bound that some block reaches.
All inputs are finite; a program needn't handle non-finite values.
Results may differ from the reference program's by a relative error of at most 0.014.
Values may be sent and summed in bfloat16 or wider, within the bound.
No kernel may reach another device: no remote copies, remote signals or barrier semaphores. Data moves between devices by JAX's collectives and lax.ppermute only.
A program may use at most 128 MiB of HBM per device.

```python
import math
import jax
import jax.numpy as jnp
import numpy as np
from jax import lax

D = 2880
TOP = 4
HID = 2048
TOK_DEV = 128
EXPERTS = 64
CAP = 16
SEQ_LEN = 4096
N_CTX = 32
N_EXP = 8


def shard_levels(stream_key, shape, cuts, least, largest):
    loudness, own = 1.0, jax.random.fold_in(stream_key, 6)
    for axis_at, blocks in cuts:
        draws = jnp.exp(jax.random.uniform(jax.random.fold_in(own, axis_at), (blocks,), jnp.float32, least / len(cuts), largest / len(cuts)))
        loudness = loudness * jnp.repeat(draws, shape[axis_at] // blocks).reshape([-1 if axis == axis_at else 1 for axis in range(len(shape))])
    return loudness


def shared_out(stream_key, own, number, rows, count, top, bound, slope):
    sequence = jax.random.permutation(stream_key, count)
    packed, common = portions_of(count, rows * top, bound, slope, True), portions_of(count, rows * top, bound, slope, False)
    places = jnp.arange(count)

    def named(tallies, rotation):
        used = int((tallies > 0).sum())
        fixed = max(1, used // 4)
        passed = fixed + (places - fixed + rotation * (used - fixed)) % max(1, count - fixed)
        return jnp.zeros((count,), jnp.int32).at[sequence[jnp.where(places < fixed, places, passed)]].set(jnp.asarray(tallies, jnp.int32))

    tallies = jnp.where(number % 4 == 0, named(packed, number // 4), named(common, number - number // 4 - 1))
    mixed = jax.random.permutation(jax.random.fold_in(own, 3), count)
    giver, sink = mixed[0:count // 2 * 2:2], mixed[1:count // 2 * 2:2]
    room = jnp.minimum(tallies[giver] - 1, bound - tallies[sink]) // 2
    room = jnp.where((giver == sequence[0]) | (sink == sequence[0]) | (tallies[sink] == 0), 0, jnp.maximum(room, 0))
    passed = jax.random.randint(jax.random.fold_in(own, 4), (count // 2,), 0, 1 << 20) % (room + 1)
    tallies = tallies.at[giver].add(-passed).at[sink].add(passed)
    items = jnp.searchsorted(jnp.cumsum(tallies), jnp.arange(rows * top), side="right").astype(jnp.int32)
    table = items.reshape(top, rows).T
    table = table[jax.random.permutation(jax.random.fold_in(own, 1), rows)]
    rotation = jax.random.randint(jax.random.fold_in(own, 2), (rows, 1), 0, top)
    return jnp.take_along_axis(table, (jnp.arange(top)[None, :] + rotation) % top, axis=1)


def portions_of(count, total, most, slope, full):
    weights = [(1 << 20) // math.isqrt(grade ** slope) + 1 for grade in range(1, count + 1)]
    largest = most if full else min(most, max(-(-total // count), total * weights[0] // sum(weights)))
    least = 1 if total - largest >= count - 1 else 0
    given, spare = [largest] + [least] * (count - 1), total - largest - least * (count - 1)
    while spare > 0:
        candidates = [i for i in range(1, count) if given[i] < largest] or [i for i in range(1, count) if given[i] < most]
        mass, budget = sum([weights[i] for i in candidates]), spare
        for i in candidates:
            extra = min(most - given[i], max(1, budget * weights[i] // mass), spare)
            given[i] = given[i] + extra
            spare = spare - extra
    return np.array(given)


def bell_draw(key, extent, width, limit, split=(), kind=jnp.bfloat16):
    entries = jax.random.normal(key, extent, jnp.float32) * width
    if len(split) > 0:
        entries = shard_levels(key, extent, split, -0.22, 0.18) * entries
    return jnp.clip(entries, min=-limit, max=limit).astype(kind)


def setup_inputs(seed: int = 0) -> dict:
    key_list = jax.random.split(jax.random.key(seed), 6)
    hidden_acts = bell_draw(key_list[0], (EXPERTS, N_CTX, CAP, HID), 1.0, 6.0, ((0, 32), (3, 8)))
    down_weight = bell_draw(key_list[1], (EXPERTS, HID, D), HID ** -0.5, 0.125, ((0, 32), (1, 8)))
    expert_ids_keys = jax.random.split(jax.random.fold_in(key_list[2], 1), SEQ_LEN // TOK_DEV)
    expert_ids_turns = jax.random.permutation(jax.random.fold_in(key_list[2], 3), SEQ_LEN // TOK_DEV)
    expert_ids = jax.vmap(lambda own, number: shared_out(jax.random.fold_in(key_list[2], 2), own, number, TOK_DEV, EXPERTS, TOP, CAP, 1))(expert_ids_keys, expert_ids_turns).reshape((SEQ_LEN, TOP))
    route_logits = bell_draw(key_list[3], (SEQ_LEN, TOP), 1.0, 4.0, ((0, 32),), jnp.float32)
    out_grad = bell_draw(key_list[4], (SEQ_LEN, D), 1.0, 6.0, ((0, 32), (1, 8)))
    return dict(hidden_acts=hidden_acts, down_weight=down_weight, expert_ids=expert_ids, route_logits=route_logits, out_grad=out_grad)


def slot_index(group_ids, expert_count):
    onehot = (group_ids[..., None] == jnp.arange(expert_count, dtype=jnp.int32)).astype(jnp.int32)
    running = jnp.cumsum(onehot, axis=1)
    return (jnp.sum(running * onehot, axis=2) - 1).astype(jnp.int32)


def reference(hidden_acts, down_weight, expert_ids, route_logits, out_grad):
    weights = jnp.exp(route_logits)
    route_probs = weights / jnp.sum(weights, axis=1, keepdims=True)
    slot_pos = slot_index(expert_ids.reshape(N_CTX, TOK_DEV * TOP), EXPERTS).reshape(SEQ_LEN, TOP)
    group_of = (jnp.arange(SEQ_LEN, dtype=jnp.int32) // TOK_DEV)[:, None]
    flat_index = ((expert_ids * N_CTX + group_of) * CAP + slot_pos).reshape(-1).astype(jnp.int32)
    block_width = HID // N_EXP

    def expert_rows(operands):
        activations, weight = operands
        act_rows = activations.reshape(N_CTX * CAP, HID)
        running_sum = jnp.zeros((N_CTX * CAP, D), jnp.float32)
        for part_index in range(N_EXP):
            first_col = part_index * block_width
            block_out = jnp.dot(act_rows[:, first_col:first_col + block_width], weight[first_col:first_col + block_width], preferred_element_type=jnp.float32).astype(jnp.bfloat16)
            running_sum = running_sum + lax.optimization_barrier(block_out).astype(jnp.float32)
        return running_sum

    expert_out = lax.map(expert_rows, (hidden_acts, down_weight))
    picked = expert_out.reshape(-1, D)[flat_index].reshape(SEQ_LEN, TOP, D)
    combined = jnp.einsum("tk,tkd->td", route_probs, picked).astype(jnp.bfloat16)
    grad_values = out_grad.astype(jnp.float32)
    prob_grad = jnp.einsum("td,tkd->tk", grad_values, picked)
    grad_logits = route_probs * (prob_grad - jnp.sum(route_probs * prob_grad, axis=1, keepdims=True))
    slot_rows = (route_probs[:, :, None] * grad_values[:, None, :]).astype(jnp.bfloat16).reshape(-1, D)
    slot_grad = jnp.zeros((EXPERTS * N_CTX * CAP, D), jnp.bfloat16).at[flat_index].set(slot_rows).reshape(EXPERTS, N_CTX * CAP, D)

    def expert_grads(operands):
        activations, weight, grad_rows = operands
        act_rows = activations.reshape(N_CTX * CAP, HID)
        grad_acts = jnp.dot(grad_rows, weight.T, preferred_element_type=jnp.float32).astype(jnp.bfloat16).reshape(N_CTX, CAP, HID)
        grad_w = jnp.dot(act_rows.T, grad_rows, preferred_element_type=jnp.float32).astype(jnp.bfloat16)
        return grad_acts, grad_w

    grad_hidden, grad_weight = lax.map(expert_grads, (hidden_acts, down_weight, slot_grad))
    return (combined, grad_logits, grad_hidden, grad_weight)
```

```python
import functools

import jax
import jax.numpy as jnp
from jax import lax
from jax.experimental import pallas as pl
from jax.experimental.pallas import tpu as pltpu
from jax.sharding import Mesh
from jax.sharding import PartitionSpec as P

EXP = ("zl", "y")
F32, BF16 = jnp.float32, jnp.bfloat16
VMEM = pl.BlockSpec(memory_space=pltpu.VMEM)


def dot(a, b, ca, cb):
    return lax.dot_general(a, b, (((ca,), (cb,)), ((), ())), preferred_element_type=F32)


def routing(ids_ref, logits_ref, experts):
    ids = ids_ref[...]
    weights = jnp.exp(logits_ref[...])
    probs = weights / jnp.sum(weights, axis=0, keepdims=True)
    top, tokens = ids.shape
    expert = lax.broadcasted_iota(jnp.int32, (experts, tokens), 0)
    named = jnp.zeros((experts, tokens), F32)
    prob = jnp.zeros((experts, tokens), F32)
    for k in range(top):
        hit = ids[k : k + 1, :] == expert
        named = jnp.where(hit, 1.0, named)
        prob = jnp.where(hit, probs[k : k + 1, :], prob)
    before = lax.broadcasted_iota(jnp.int32, (tokens, tokens), 0)
    after = lax.broadcasted_iota(jnp.int32, (tokens, tokens), 1)
    earlier = jnp.where(before < after, 1.0, 0.0).astype(BF16)
    place = dot(named.astype(BF16), earlier, 1, 0)
    slot = jnp.where(named > 0, place, -1.0)
    return ids, probs, prob, slot


def placed(slot, values, capacity):
    experts, tokens = slot.shape
    s = lax.broadcasted_iota(jnp.int32, (experts, capacity, tokens), 1).astype(F32)
    full = jnp.where(slot[:, None, :] == s, values[:, None, :], 0.0)
    return full.reshape(experts * capacity, tokens)


def split(x):
    high = x.astype(BF16)
    return high, (x - high.astype(F32)).astype(BF16)


def dispatch_kernel(experts, capacity, ids_ref, logits_ref, grad_ref, out_ref):
    _, _, prob, slot = routing(ids_ref, logits_ref, experts)
    high, low = split(placed(slot, prob, capacity))
    g = grad_ref[...]
    rows = dot(high, g, 1, 1) + dot(low, g, 1, 1)
    out_ref[...] = rows.astype(BF16).reshape(out_ref.shape)


def combine_kernel(experts, capacity, ids_ref, logits_ref, grad_ref, rows_ref, out_ref, part_ref, probs_ref):
    ids, probs, prob, slot = routing(ids_ref, logits_ref, experts)
    tokens = ids.shape[1]
    high, low = split(placed(slot, prob, capacity))
    rows = rows_ref[...].reshape(experts * capacity, rows_ref.shape[-1])
    out_ref[...] = (dot(rows, high, 0, 0) + dot(rows, low, 0, 0)).astype(BF16)
    q = dot(rows, grad_ref[...], 1, 0)
    mask = placed(slot, jnp.ones_like(slot), capacity)
    per_expert = jnp.sum((q * mask).reshape(experts, capacity, tokens), axis=1)
    expert = lax.broadcasted_iota(jnp.int32, (experts, tokens), 0)
    for k in range(ids.shape[0]):
        hit = ids[k : k + 1, :] == expert
        part_ref[k : k + 1, :] = jnp.sum(jnp.where(hit, per_expert, 0.0), axis=0, keepdims=True)
    probs_ref[...] = probs


def partial_kernel(halved, order_ref, hidden_ref, weight_ref, *out_refs):
    experts, groups, slots, width = hidden_ref.shape
    step = pl.program_id(0)
    at = 0
    for k, cut in enumerate(halved):
        refs = out_refs[at : at + 1 + cut]
        at += 1 + cut

        @pl.when(step == k)
        def _(refs=refs):
            for e in range(experts):
                h = hidden_ref[e].reshape(groups * slots, width)
                out = dot(h, weight_ref[e, 0], 1, 1).astype(BF16)
                out = out.reshape(groups, slots, out.shape[-1])
                first = 0
                for ref in refs:
                    ref[:, e] = out[first : first + ref.shape[0]]
                    first += ref.shape[0]


def partial_blocks(order, halved, hidden, weight):
    experts, groups, slots, width = hidden.shape
    d = weight.shape[2]
    shapes = []
    for cut in halved:
        shapes += [jax.ShapeDtypeStruct((groups // (1 + cut), experts, slots, d), BF16)] * (1 + cut)
    return pl.pallas_call(
        functools.partial(partial_kernel, halved),
        out_shape=shapes,
        grid_spec=pltpu.PrefetchScalarGridSpec(
            num_scalar_prefetch=1,
            grid=(len(halved),),
            in_specs=[
                pl.BlockSpec(hidden.shape, lambda i, o: (0, 0, 0, 0)),
                pl.BlockSpec((experts, 1, d, width), lambda i, o: (0, o[i], 0, 0)),
            ],
            out_specs=[pl.BlockSpec(s.shape, lambda i, o: (0, 0, 0, 0)) for s in shapes],
        ),
        name="partial_blocks",
    )(order, hidden, weight)


def grads_kernel(halved, first, last, order_ref, hidden_ref, weight_ref, *refs):
    experts, groups, slots, width = hidden_ref.shape
    refs = list(refs)
    blocks = []
    for cut in halved:
        blocks.append([refs.pop(0) for _ in range(1 + cut)])
    if not first:
        carry_ref = refs.pop(0)
        refs.pop(0)
    gh_ref, gw_ref, total_ref = refs
    step = pl.program_id(0)

    @pl.when(step == 0)
    def _():
        if first:
            total_ref[...] = jnp.zeros_like(total_ref)
        else:
            total_ref[...] = carry_ref[...]

    for k, parts in enumerate(blocks):

        @pl.when(step == k)
        def _(parts=parts):
            for e in range(experts):
                x = [p[:, e] for p in parts]
                x = x[0] if len(x) == 1 else jnp.concatenate(x, axis=0)
                x = x.reshape(groups * slots, x.shape[-1])
                h = hidden_ref[e].reshape(groups * slots, width)
                total_ref[e] += dot(x, weight_ref[e, 0], 1, 0)
                gw_ref[e, 0] = dot(x, h, 0, 0).astype(BF16)

    @pl.when(step == len(blocks) - 1)
    def _():
        if last:
            gh_ref[...] = total_ref[...].astype(BF16).reshape(gh_ref.shape)
        else:
            gh_ref[...] = total_ref[...]


def grads(order, halved, hidden, weight, blocks, carry=None, gw=None, last=True):
    experts, groups, slots, width = hidden.shape
    exp, d = weight.shape[1], weight.shape[2]
    first = carry is None
    wblock = pl.BlockSpec((experts, 1, d, width), lambda i, o: (0, o[i], 0, 0))
    whole = lambda a: pl.BlockSpec(a.shape, lambda i, o: (0,) * len(a.shape))
    total = jax.ShapeDtypeStruct((experts, groups * slots, width), F32)
    gh = jax.ShapeDtypeStruct(hidden.shape, BF16) if last else total
    args = [order, hidden, weight, *blocks]
    specs = [whole(hidden), wblock] + [whole(b) for b in blocks]
    aliases = {}
    if not first:
        args += [carry, gw]
        specs += [whole(carry), pl.BlockSpec(memory_space=pl.ANY)]
        aliases = {len(args) - 1: 1}
    return pl.pallas_call(
        functools.partial(grads_kernel, halved, first, last),
        out_shape=[gh, jax.ShapeDtypeStruct(weight.shape, BF16)],
        grid_spec=pltpu.PrefetchScalarGridSpec(
            num_scalar_prefetch=1,
            grid=(len(halved),),
            in_specs=specs,
            out_specs=[whole(gh), wblock],
            scratch_shapes=[pltpu.VMEM(total.shape, F32)],
        ),
        input_output_aliases=aliases,
        name="grads",
    )(*args)


def shifted(x, axis, by):
    n = lax.axis_size(axis)
    return lax.ppermute(x, axis, [(i, (i + by) % n) for i in range(n)])


def added(*xs):
    return functools.reduce(lambda a, b: a + b, [x.astype(F32) for x in xs]).astype(BF16)


def local(hidden_acts, down_weight, expert_ids, route_logits, out_grad):
    ctx = lax.axis_size("ctx")
    ny, nz = lax.axis_size("y"), lax.axis_size("zl")
    y, z = lax.axis_index("y"), lax.axis_index("zl")
    held, groups, capacity, width = hidden_acts.shape
    experts = held * ctx
    d = out_grad.shape[1]
    tokens = expert_ids.shape[0]
    ids, logits, grad = expert_ids.T, route_logits.T, out_grad.T
    weight = down_weight.reshape(held, width, ny * nz, d).transpose(0, 2, 3, 1)

    def at(dy, dz):
        return ((z + dz) % nz) * ny + (y + dy) % ny

    up = lambda x: shifted(x, "y", 1)
    down = lambda x: shifted(x, "y", -1)
    over = lambda x: shifted(x, "zl", 1)

    slot_rows = pl.pallas_call(
        functools.partial(dispatch_kernel, experts, capacity),
        out_shape=jax.ShapeDtypeStruct((ctx, held, capacity, d), BF16),
        in_specs=[VMEM] * 3,
        out_specs=VMEM,
        name="dispatch",
    )(ids, logits, grad)
    own = lax.all_to_all(slot_rows, "ctx", 0, 0, tiled=True)

    far_up, far_down, far_two = partial_blocks(
        jnp.stack([at(1, 1), at(-1, 1), at(2, 1)]).astype(jnp.int32), (0, 0, 0), hidden_acts, weight
    )
    r_far_up, r_far_down, r_far_two = up(far_up), down(far_down), over(far_two)
    two_lo, two_hi, up_lo, up_hi, down_lo, down_hi, far_own, near_own = partial_blocks(
        jnp.stack([at(2, 0), at(1, 0), at(-1, 0), at(0, 1), at(0, 0)]).astype(jnp.int32),
        (1, 1, 1, 0, 0),
        hidden_acts,
        weight,
    )
    r_up_hi, r_down_lo = up(up_hi), down(down_lo)
    half = groups // 2
    r_two_lo = up(added(two_lo, r_far_two[:half]))
    r_two_hi = down(added(two_hi, r_far_two[half:]))
    r_own = over(added(far_own, r_far_up, r_far_down))
    r_up_lo = up(added(up_lo, r_two_lo))
    r_down_hi = down(added(down_hi, r_two_hi))
    summed = added(
        near_own,
        jnp.concatenate([r_up_lo, r_up_hi], axis=0),
        jnp.concatenate([r_down_lo, r_down_hi], axis=0),
        r_own,
    )
    returned = lax.all_to_all(summed, "ctx", 0, 0, tiled=True)
    combined, part, probs = pl.pallas_call(
        functools.partial(combine_kernel, experts, capacity),
        out_shape=[
            jax.ShapeDtypeStruct((d, tokens), BF16),
            jax.ShapeDtypeStruct(ids.shape, F32),
            jax.ShapeDtypeStruct(ids.shape, F32),
        ],
        in_specs=[VMEM] * 4,
        out_specs=[VMEM] * 3,
        name="combine",
    )(ids, logits, grad, returned)
    part = part + over(part)
    part = part + lax.ppermute(part, "y", [(i, i ^ 1) for i in range(ny)])
    part = part + lax.ppermute(part, "y", [(i, i ^ 2) for i in range(ny)])
    grad_logits = probs * (part - jnp.sum(probs * part, axis=0, keepdims=True))

    own_lo, own_hi = own[:half], own[half:]
    a_lo, b_hi = up(own_lo), down(own_hi)
    a_hi, b_lo = up(own_hi), down(own_lo)
    c = over(own)
    d_lo, d_hi = up(a_lo), down(b_hi)
    fa, fb = up(c), down(c)
    fd_lo, fd_hi = over(d_lo), over(d_hi)
    carry, gw = grads(
        jnp.stack([at(0, 0), at(-1, 0), at(1, 0), at(0, 1)]).astype(jnp.int32),
        (0, 1, 1, 0),
        hidden_acts,
        weight,
        [own, a_lo, a_hi, b_lo, b_hi, c],
        last=False,
    )
    grad_hidden, gw = grads(
        jnp.stack([at(2, 0), at(-1, 1), at(1, 1), at(2, 1)]).astype(jnp.int32),
        (1, 0, 0, 1),
        hidden_acts,
        weight,
        [d_lo, d_hi, fa, fb, fd_lo, fd_hi],
        carry,
        gw,
    )
    grad_weight = gw.transpose(0, 3, 1, 2).reshape(down_weight.shape)
    return (combined.T, grad_logits.T, grad_hidden, grad_weight)


def solution(mesh):
    torus = Mesh(mesh.devices.reshape(mesh.shape["ctx"], 2, 4), ("ctx", "zl", "y"))
    return jax.shard_map(
        local,
        mesh=torus,
        in_specs=(
            P("ctx", None, None, EXP),
            P("ctx", EXP, None),
            P("ctx", None),
            P("ctx", None),
            P("ctx", EXP),
        ),
        out_specs=(P("ctx", EXP), P("ctx", None), P("ctx", None, None, EXP), P("ctx", EXP, None)),
        check_vma=False,
    )
```
